32 devices in a mesh: section: 2 (over y), expert: 4 (over z), hid: 4 (over x, core).
Axes of the slice: x: 2, y: 2, z: 4, core: 2. Of those that a mesh axis runs over, the one named last changes fastest.
Arguments:
- saved_input: bfloat16 [2, 512, 4096], P('section', 'expert', 'hid'), may hold values from -6 to 6
- cotangent: bfloat16 [2, 512, 4096], P('section', 'expert', 'hid'), may hold values from -6 to 6
- next_input: bfloat16 [2, 512, 4096], P('section', 'expert', 'hid'), may hold values from -6 to 6
- routes_saved: int32 [2, 512, 2], P('section', 'expert'), may hold values from 0 to 3, all different within a row; in each aligned block of 128 rows (0 to 127, 128 to 255, ..., all dimensions but the last counted through in order) at most 96 rows name the same one
- routes_next: int32 [2, 512, 2], P('section', 'expert'), may hold values from 0 to 3, all different within a row; in each aligned block of 128 rows (0 to 127, 128 to 255, ..., all dimensions but the last counted through in order) at most 96 rows name the same one
- norm_gain: float32 [2, 4096], P('section', 'hid'), may hold values from 0.1 to 1.9
- router: float32 [2, 4096, 4], P('section', 'hid'), may hold values from -0.18 to 0.18
- expert_gate: bfloat16 [2, 4, 4096, 7168], P('section', 'expert', None, 'hid'), may hold values from -0.09375 to 0.09375
- expert_up: bfloat16 [2, 4, 4096, 7168], P('section', 'expert', None, 'hid'), may hold values from -0.09375 to 0.09375
- expert_down: bfloat16 [2, 4, 7168, 4096], P('section', 'expert', 'hid'), may hold values from -0.0625 to 0.0625
Outputs:
- leaving: bfloat16 [2, 512, 4096], P('section', 'expert', 'hid')
- arriving: bfloat16 [2, 512, 4096], P('section', 'expert', 'hid')
The draws below stay inside these ranges and needn't reach their ends.
Inputs may be any that keep to these rules, and one draw needn't show every extreme that they name: `routes_saved`: A token's two ids differ. In each aligned block of 128 tokens of a section no expert is named by more than 96 tokens, and some block names some expert exactly 96 times. `routes_next`: A token's two ids differ. In each aligned block of 128 tokens of a section no expert is named by more than 96 tokens, and some block names some expert exactly 96 times.
All inputs are finite; a program needn't handle non-finite values.
Results may differ from the reference program's by a relative error of at most 0.0052.
Values may be sent and summed in bfloat16 or wider, within the bound.
A program may use at most 128 MiB of HBM per device.

```python
import math
import jax
import jax.numpy as jnp
import numpy as np
from jax import lax

D = 4096
FF = 7168
TOK_DEV = 128
EXPERTS = 4
CAP = 96
TOKENS = 512
N_SECTION = 2
N_EXPERT = 4


def block_levels(key, shape, split, low, top_value):
    factor_of, own = 1.0, jax.random.fold_in(key, 6)
    for position, blocks in split:
        heights = jnp.exp(jax.random.uniform(jax.random.fold_in(own, position), (blocks,), jnp.float32, low / len(split), top_value / len(split)))
        factor_of = factor_of * jnp.repeat(heights, shape[position] // blocks).reshape([-1 if axis == position else 1 for axis in range(len(shape))])
    return factor_of


def shared_out(rng, own, number, rows, count, top, reach, lean):
    ranking = jax.random.permutation(rng, count)
    crowded, ordinary = portions_of(count, rows * top, reach, lean, True), portions_of(count, rows * top, reach, lean, False)
    places = jnp.arange(count)

    def named(tallies, offset_by):
        used = int((tallies > 0).sum())
        fixed = max(1, used // 4)
        passed = fixed + (places - fixed + offset_by * (used - fixed)) % max(1, count - fixed)
        return jnp.zeros((count,), jnp.int32).at[ranking[jnp.where(places < fixed, places, passed)]].set(jnp.asarray(tallies, jnp.int32))

    tallies = jnp.where(number % 4 == 0, named(crowded, number // 4), named(ordinary, number - number // 4 - 1))
    mixed = jax.random.permutation(jax.random.fold_in(own, 3), count)
    source_of, taker = mixed[0:count // 2 * 2:2], mixed[1:count // 2 * 2:2]
    margin = jnp.minimum(tallies[source_of] - 1, reach - tallies[taker]) // 2
    margin = jnp.where((source_of == ranking[0]) | (taker == ranking[0]) | (tallies[taker] == 0), 0, jnp.maximum(margin, 0))
    passed = jax.random.randint(jax.random.fold_in(own, 4), (count // 2,), 0, 1 << 20) % (margin + 1)
    tallies = tallies.at[source_of].add(-passed).at[taker].add(passed)
    items = jnp.searchsorted(jnp.cumsum(tallies), jnp.arange(rows * top), side="right").astype(jnp.int32)
    table = items.reshape(top, rows).T
    table = table[jax.random.permutation(jax.random.fold_in(own, 1), rows)]
    offset_by = jax.random.randint(jax.random.fold_in(own, 2), (rows, 1), 0, top)
    return jnp.take_along_axis(table, (jnp.arange(top)[None, :] + offset_by) % top, axis=1)


def portions_of(amount, total, reach, slope, full):
    weights = [(1 << 20) // math.isqrt(grade ** slope) + 1 for grade in range(1, amount + 1)]
    largest = reach if full else min(reach, max(-(-total // amount), total * weights[0] // sum(weights)))
    least = 1 if total - largest >= amount - 1 else 0
    holding, spare = [largest] + [least] * (amount - 1), total - largest - least * (amount - 1)
    while spare > 0:
        candidates = [i for i in range(1, amount) if holding[i] < largest] or [i for i in range(1, amount) if holding[i] < reach]
        pool, left = sum([weights[i] for i in candidates]), spare
        for i in candidates:
            more = min(reach - holding[i], max(1, left * weights[i] // pool), spare)
            holding[i] = holding[i] + more
            spare = spare - more
    return np.array(holding)


def normal_values(stream_key, extent, spread, limit, pieces=(), kind=jnp.bfloat16):
    drawn = jax.random.normal(stream_key, extent, jnp.float32) * spread
    if len(pieces) > 0:
        drawn = block_levels(stream_key, extent, pieces, -0.22, 0.18) * drawn
    return jnp.clip(drawn, min=-limit, max=limit).astype(kind)


def setup_inputs(seed: int = 0) -> dict:
    key_of = jax.random.split(jax.random.key(seed), 11)
    saved_input = normal_values(key_of[0], (N_SECTION, TOKENS, D), 1.0, 6.0, ((0, 2), (1, 4), (2, 4)))
    cotangent = normal_values(key_of[1], (N_SECTION, TOKENS, D), 1.0, 6.0, ((0, 2), (1, 4), (2, 4)))
    next_input = normal_values(key_of[2], (N_SECTION, TOKENS, D), 1.0, 6.0, ((0, 2), (1, 4), (2, 4)))
    routes_saved_keys = jax.random.split(jax.random.fold_in(key_of[3], 1), N_SECTION * TOKENS // TOK_DEV)
    routes_saved_turns = jax.random.permutation(jax.random.fold_in(key_of[3], 3), N_SECTION * TOKENS // TOK_DEV)
    routes_saved = jax.vmap(lambda own, number: shared_out(jax.random.fold_in(key_of[3], 2), own, number, TOK_DEV, EXPERTS, 2, CAP, 1))(routes_saved_keys, routes_saved_turns).reshape((N_SECTION, TOKENS, 2))
    routes_next_keys = jax.random.split(jax.random.fold_in(key_of[4], 1), N_SECTION * TOKENS // TOK_DEV)
    routes_next_turns = jax.random.permutation(jax.random.fold_in(key_of[4], 3), N_SECTION * TOKENS // TOK_DEV)
    routes_next = jax.vmap(lambda own, number: shared_out(jax.random.fold_in(key_of[4], 2), own, number, TOK_DEV, EXPERTS, 2, CAP, 1))(routes_next_keys, routes_next_turns).reshape((N_SECTION, TOKENS, 2))
    norm_gain = jnp.clip(1.0 + 0.18 * jax.random.normal(key_of[5], (N_SECTION, D), jnp.float32), 0.1, 1.9)
    router = normal_values(key_of[6], (N_SECTION, D, EXPERTS), 0.03, 0.18, ((0, 2), (1, 4)), jnp.float32)
    expert_gate = normal_values(key_of[7], (N_SECTION, EXPERTS, D, FF), D ** -0.5, 0.09375, ((0, 2), (1, 4), (3, 4)))
    expert_up = normal_values(key_of[8], (N_SECTION, EXPERTS, D, FF), D ** -0.5, 0.09375, ((0, 2), (1, 4), (3, 4)))
    expert_down = normal_values(key_of[9], (N_SECTION, EXPERTS, FF, D), FF ** -0.5, 0.0625, ((0, 2), (1, 4), (2, 4)))
    return {"saved_input": saved_input, "cotangent": cotangent, "next_input": next_input, "routes_saved": routes_saved, "routes_next": routes_next, "norm_gain": norm_gain, "router": router, "expert_gate": expert_gate, "expert_up": expert_up, "expert_down": expert_down}


EPSILON = 1e-05
HIGHEST = lax.Precision.HIGHEST

def norm_stats(inputs, gain, table):
    values = inputs.astype(jnp.float32)
    scale = lax.rsqrt(lax.optimization_barrier(jnp.sum(values * values, axis=1)) / D + EPSILON)
    scaled = values * scale[:, None] * gain[None, :]
    logits = jnp.dot(scaled, table, precision=HIGHEST)
    return (values, scale, scaled.astype(jnp.bfloat16), logits)

def placing(routes, logits):
    labels = jnp.arange(EXPERTS, dtype=jnp.int32)
    blocks = routes.reshape(N_EXPERT, TOK_DEV * 2).astype(jnp.int32)
    onehot = (blocks[:, :, None] == labels[None, None, :]).astype(jnp.int32)
    ranked = (jnp.cumsum(onehot, axis=1) - onehot).astype(jnp.int32)
    places = lax.optimization_barrier(jnp.sum(ranked * onehot, axis=2)).astype(jnp.int32)
    anchor = jnp.arange(N_EXPERT, dtype=jnp.int32)[:, None]
    targets = (blocks * (N_EXPERT * CAP) + anchor * CAP + places).astype(jnp.int32).reshape(TOKENS, 2)
    first_hit = (routes[:, 0:1] == labels[None, :]).astype(jnp.float32)
    second_hit = (routes[:, 1:2] == labels[None, :]).astype(jnp.float32)
    first_logit = lax.optimization_barrier(jnp.sum(logits * first_hit, axis=1))
    second_logit = lax.optimization_barrier(jnp.sum(logits * second_hit, axis=1))
    first_prob = jax.nn.sigmoid(first_logit - second_logit)
    second_prob = jax.nn.sigmoid(second_logit - first_logit)
    return (targets, first_prob, second_prob, first_hit - second_hit)

def spread_rows(targets, rows):
    total = EXPERTS * N_EXPERT * CAP
    doubled = jnp.repeat(rows, 2, axis=0)
    filled = jnp.zeros((total, rows.shape[1]), rows.dtype).at[targets.reshape(-1)].set(doubled)
    return filled.reshape(EXPERTS, N_EXPERT * CAP, rows.shape[1])

def blend(rows, targets, first_prob, second_prob):
    return first_prob[:, None] * rows[targets[:, 0]] + second_prob[:, None] * rows[targets[:, 1]]

def expert_rows(packed):
    saved_rows, cot_rows, next_rows, gate_matrix, up_matrix, down_matrix = packed
    gate_saved = jnp.dot(saved_rows, gate_matrix, preferred_element_type=jnp.float32)
    up_saved = jnp.dot(saved_rows, up_matrix, preferred_element_type=jnp.float32)
    grad_hidden = jnp.dot(cot_rows, down_matrix.T, preferred_element_type=jnp.float32)
    sig_saved = jax.nn.sigmoid(gate_saved)
    silu_saved = gate_saved * sig_saved
    hidden_saved = (silu_saved * up_saved).astype(jnp.bfloat16)
    row_dots = lax.optimization_barrier(jnp.sum(grad_hidden * hidden_saved.astype(jnp.float32), axis=1))
    grad_gate = (grad_hidden * up_saved * (sig_saved * (1.0 + gate_saved * (1.0 - sig_saved)))).astype(jnp.bfloat16)
    grad_up = (grad_hidden * silu_saved).astype(jnp.bfloat16)
    back_rows = jnp.dot(grad_gate, gate_matrix.T, preferred_element_type=jnp.float32) + jnp.dot(grad_up, up_matrix.T, preferred_element_type=jnp.float32)
    gate_next = jnp.dot(next_rows, gate_matrix, preferred_element_type=jnp.float32)
    up_next = jnp.dot(next_rows, up_matrix, preferred_element_type=jnp.float32)
    silu_next = gate_next * jax.nn.sigmoid(gate_next)
    hidden_next = (silu_next * up_next).astype(jnp.bfloat16)
    out_rows = jnp.dot(hidden_next, down_matrix, preferred_element_type=jnp.float32)
    return (back_rows, row_dots, out_rows)

def section_pass(saved, cotangent, upcoming, routes_saved, routes_next, gain, table, gate_all, up_all, down_all):
    values_saved, scale_saved, normed_saved, logits_saved = norm_stats(saved, gain, table)
    values_next, scale_next, normed_next, logits_next = norm_stats(upcoming, gain, table)
    targets_saved, first_saved, second_saved, diff_saved = placing(routes_saved, logits_saved)
    targets_next, first_next, second_next, diff_next = placing(routes_next, logits_next)
    buffer_saved = spread_rows(targets_saved, normed_saved)
    buffer_cot = spread_rows(targets_saved, cotangent)
    buffer_next = spread_rows(targets_next, normed_next)
    back_rows, row_dots, out_rows = lax.map(expert_rows, (buffer_saved, buffer_cot, buffer_next, gate_all, up_all, down_all))
    total = EXPERTS * N_EXPERT * CAP
    back_rows = back_rows.reshape(total, D)
    row_dots = row_dots.reshape(total)
    out_rows = out_rows.reshape(total, D)
    branch_next = blend(out_rows, targets_next, first_next, second_next)
    forward_out = (values_next + branch_next).astype(jnp.bfloat16)
    mixed_saved = blend(back_rows, targets_saved, first_saved, second_saved)
    grad_logit = (row_dots[targets_saved[:, 0]] - row_dots[targets_saved[:, 1]]) * first_saved * second_saved
    grad_normed = mixed_saved + jnp.dot(grad_logit[:, None] * diff_saved, table.T, precision=HIGHEST)
    scaled_grad = grad_normed * gain[None, :]
    inner = lax.optimization_barrier(jnp.sum(scaled_grad * values_saved, axis=1))
    cube = scale_saved * scale_saved * scale_saved
    grad_input = cotangent.astype(jnp.float32) + scale_saved[:, None] * scaled_grad - values_saved * cube[:, None] * (inner / D)[:, None]
    return (forward_out, grad_input.astype(jnp.bfloat16))

def reference(saved_input, cotangent, next_input, routes_saved, routes_next, norm_gain, router, expert_gate, expert_up, expert_down):
    forward_outs = []
    grad_inputs = []
    for section_index in range(N_SECTION):
        forward_out, grad_input = section_pass(saved_input[section_index], cotangent[section_index], next_input[section_index], routes_saved[section_index], routes_next[section_index], norm_gain[section_index], router[section_index], expert_gate[section_index], expert_up[section_index], expert_down[section_index])
        forward_outs.append(forward_out)
        grad_inputs.append(grad_input)
    leaving = jnp.stack([grad_inputs[0], forward_outs[1]])
    arriving = jnp.stack([grad_inputs[1], forward_outs[0]])
    return (leaving, arriving)
```

```python
import jax
import jax.numpy as jnp
from jax import lax
from jax.sharding import PartitionSpec as P

EPSILON = 1e-05
HIGHEST = lax.Precision.HIGHEST
CONTRACT = (((1,), (1,)), ((), ()))
LEADING = (((0,), (0,)), ((), ()))
F32 = jnp.float32
BF16 = jnp.bfloat16


def bits_of(count):
    return [1 << bit for bit in range(count.bit_length() - 1)]


def swap(block, axis, step):
    count = lax.axis_size(axis)
    return lax.ppermute(block, axis, [(i, i ^ step) for i in range(count)])


def one_way(block, axis, source, target):
    return lax.ppermute(block, axis, [(source, target)])


def butterfly_sum(block, axis):
    for step in bits_of(lax.axis_size(axis)):
        block = block + swap(block, axis, step)
    return block


def pick(choices, index, steps):
    if not steps:
        return choices[0]
    step = steps[-1]
    low = pick(choices[:step], index, steps[:-1])
    high = pick(choices[step:], index, steps[:-1])
    return jnp.where((index & step) == 0, low, high)


def gather_features(block, axis):
    count = lax.axis_size(axis)
    steps = bits_of(count)
    me = lax.axis_index(axis)
    pieces = {0: block}
    for step in reversed(steps):
        arrived = {key | step: swap(piece, axis, step) for key, piece in pieces.items()}
        pieces.update(arrived)
    listed = [pieces[key] for key in range(count)]
    ordered = [pick(listed, me ^ j, steps) for j in range(count)]
    return jnp.concatenate(ordered, axis=1)


def reduce_features(partial_rows, axis):
    count = lax.axis_size(axis)
    me = lax.axis_index(axis)
    width = partial_rows.shape[1] // count
    held = [partial_rows[:, j * width:(j + 1) * width] for j in range(count)]
    for step in bits_of(count):
        clear = (me & step) == 0
        kept = []
        for low, high in zip(held[0::2], held[1::2]):
            sent = jnp.where(clear, high, low).astype(BF16)
            kept.append((jnp.where(clear, low, high), swap(sent, axis, step)))
        held = [mine + theirs.astype(F32) for mine, theirs in kept]
    return held[0]


def norm_stats(tokens, gain, table):
    values = tokens.astype(F32)
    squares = jnp.sum(values * values, axis=1)[None, :]
    scores = lax.dot_general(
        (table * gain[:, None]), values, (((0,), (1,)), ((), ())), precision=HIGHEST
    )
    totals = butterfly_sum(jnp.concatenate([squares, scores], axis=0), "hid")
    return totals[0], totals[1:]


def finish_norm(tokens, squares, scores, gain, width):
    scale = lax.rsqrt(squares / width + EPSILON)
    normed = (tokens.astype(F32) * scale[:, None] * gain[None, :]).astype(BF16)
    return scale, normed, scores * scale[None, :]


def row_map(routes, rows):
    me = lax.axis_index("expert")
    tokens = routes.shape[1]
    hit = jnp.any(routes == me, axis=0)
    before = jnp.arange(tokens)[:, None] < jnp.arange(tokens)[None, :]
    rank = jnp.dot(hit.astype(BF16)[None, :], before.astype(BF16), preferred_element_type=F32)
    rank = rank.astype(jnp.int32)
    chosen = (jnp.arange(rows, dtype=jnp.int32)[:, None] == rank) & hit[None, :]
    return chosen


def pair_terms(routes, logits):
    experts = logits.shape[0]
    labels = jnp.arange(experts, dtype=jnp.int32)[:, None]
    first_hit = (routes[0:1] == labels).astype(F32)
    second_hit = (routes[1:2] == labels).astype(F32)
    first_logit = jnp.sum(logits * first_hit, axis=0)
    second_logit = jnp.sum(logits * second_hit, axis=0)
    first_prob = jax.nn.sigmoid(first_logit - second_logit)
    second_prob = jax.nn.sigmoid(second_logit - first_logit)
    return first_prob, second_prob, first_hit - second_hit


def per_row(chosen, per_token):
    return jnp.sum(jnp.where(chosen, per_token[None, :], 0.0), axis=1)


def select_rows(chosen, tokens):
    return jnp.dot(chosen.astype(BF16), tokens, preferred_element_type=F32).astype(BF16)


def send_home(chosen, rows):
    placed = lax.dot_general(
        chosen.astype(BF16), rows.astype(BF16), LEADING, preferred_element_type=F32
    ).astype(BF16)
    return lax.psum_scatter(placed, "expert", scatter_dimension=0, tiled=True)


def per_device(
    saved_input,
    cotangent,
    next_input,
    routes_saved,
    routes_next,
    norm_gain,
    router,
    expert_gate,
    expert_up,
    expert_down,
):
    gain = norm_gain[0]
    table = router[0]
    gate_matrix = expert_gate[0, 0]
    up_matrix = expert_up[0, 0]
    down_matrix = expert_down[0, 0]
    width = gate_matrix.shape[0]
    count = saved_input.shape[1]
    rows = 3 * count * lax.axis_size("expert") // table.shape[1]
    me = lax.axis_index("expert")

    packed = jnp.concatenate([routes_saved[0].T, routes_next[0].T], axis=0)
    routes = lax.all_gather(packed, "expert", axis=1, tiled=True)
    all_cot = lax.all_gather(cotangent[0], "expert", axis=0, tiled=True)
    all_saved = lax.all_gather(saved_input[0], "expert", axis=0, tiled=True)
    all_next = lax.all_gather(next_input[0], "expert", axis=0, tiled=True)

    pair_saved, pair_next = routes[0:2], routes[2:4]
    chosen_saved = row_map(pair_saved, rows)
    chosen_next = row_map(pair_next, rows)

    cot_rows = gather_features(select_rows(chosen_saved, all_cot), "hid")
    grad_hidden = lax.dot_general(cot_rows, down_matrix, CONTRACT, preferred_element_type=F32)

    squares, scores = norm_stats(all_saved, gain, table)
    scale_saved, normed, logits = finish_norm(all_saved, squares, scores, gain, width)
    first_saved, second_saved, diff_saved = pair_terms(pair_saved, logits)
    saved_rows = gather_features(select_rows(chosen_saved, normed), "hid")

    squares, scores = norm_stats(all_next, gain, table)
    scale_next, normed, logits = finish_norm(all_next, squares, scores, gain, width)
    first_next, second_next, _ = pair_terms(pair_next, logits)
    next_rows = gather_features(select_rows(chosen_next, normed), "hid")

    gate = jnp.dot(saved_rows, gate_matrix, preferred_element_type=F32)
    up = jnp.dot(saved_rows, up_matrix, preferred_element_type=F32)
    sig = jax.nn.sigmoid(gate)
    silu = gate * sig
    hidden = (silu * up).astype(BF16)
    dots = butterfly_sum(jnp.sum(grad_hidden * hidden.astype(F32), axis=1), "hid")
    grad_gate = (grad_hidden * up * (sig * (1.0 + gate * (1.0 - sig)))).astype(BF16)
    grad_up = (grad_hidden * silu).astype(BF16)
    back_part = lax.dot_general(
        grad_gate, gate_matrix, CONTRACT, preferred_element_type=F32
    ) + lax.dot_general(grad_up, up_matrix, CONTRACT, preferred_element_type=F32)
    back = reduce_features(back_part, "hid")
    is_first = pair_saved[0] == me
    weight = per_row(chosen_saved, jnp.where(is_first, first_saved, second_saved))
    product = first_saved * second_saved
    slope = per_row(chosen_saved, jnp.where(is_first, product, -product)) * dots
    leaning = lax.dot_general(diff_saved * 1.0, table, (((0,), (1,)), ((), ())), precision=HIGHEST)
    spread = jnp.dot(chosen_saved.astype(F32), leaning, precision=HIGHEST)
    home = send_home(chosen_saved, weight[:, None] * back + slope[:, None] * spread)

    gate = jnp.dot(next_rows, gate_matrix, preferred_element_type=F32)
    up = jnp.dot(next_rows, up_matrix, preferred_element_type=F32)
    hidden = (gate * jax.nn.sigmoid(gate) * up).astype(BF16)
    out_part = jnp.dot(hidden, down_matrix, preferred_element_type=F32)
    out = reduce_features(out_part, "hid")
    weight = per_row(chosen_next, jnp.where(pair_next[0] == me, first_next, second_next))
    branch = send_home(chosen_next, weight[:, None] * out)

    values_saved = saved_input[0].astype(F32)
    scaled_grad = home.astype(F32) * gain[None, :]
    inner = butterfly_sum(jnp.sum(scaled_grad * values_saved, axis=1), "hid")
    scale = lax.dynamic_slice(scale_saved, (me * count,), (count,))
    cube = scale * scale * scale
    grad_input = (
        cotangent[0].astype(F32)
        + scale[:, None] * scaled_grad
        - values_saved * cube[:, None] * (inner / width)[:, None]
    ).astype(BF16)
    forward_out = (next_input[0].astype(F32) + branch.astype(F32)).astype(BF16)

    first_section = lax.axis_index("section") == 0
    grad_there = one_way(grad_input, "section", 1, 0)
    out_there = one_way(forward_out, "section", 0, 1)
    leaving = jnp.where(first_section, grad_input, forward_out)
    arriving = jnp.where(first_section, grad_there, out_there)
    return (leaving[None], arriving[None])


def solution(mesh):
    placed = (
        P("section", "expert", "hid"),
        P("section", "expert", "hid"),
        P("section", "expert", "hid"),
        P("section", "expert", None),
        P("section", "expert", None),
        P("section", "hid"),
        P("section", "hid", None),
        P("section", "expert", None, "hid"),
        P("section", "expert", None, "hid"),
        P("section", "expert", "hid", None),
    )
    return jax.shard_map(
        per_device,
        mesh=mesh,
        in_specs=placed,
        out_specs=(P("section", "expert", "hid"), P("section", "expert", "hid")),
        check_vma=False,
    )
```

```python
import jax
import jax.numpy as jnp
from jax import lax
from jax.sharding import PartitionSpec as P

EPSILON = 1e-05
HIGHEST = lax.Precision.HIGHEST
CONTRACT = (((1,), (1,)), ((), ()))
LEADING = (((0,), (0,)), ((), ()))
F32 = jnp.float32
BF16 = jnp.bfloat16


def bits_of(count):
    return [1 << bit for bit in range(count.bit_length() - 1)]


def swap(block, axis, step):
    count = lax.axis_size(axis)
    return lax.ppermute(block, axis, [(i, i ^ step) for i in range(count)])


def one_way(block, axis, source, target):
    return lax.ppermute(block, axis, [(source, target)])


def butterfly_sum(block, axis):
    for step in bits_of(lax.axis_size(axis)):
        block = block + swap(block, axis, step)
    return block


def pick(choices, index, steps):
    if not steps:
        return choices[0]
    step = steps[-1]
    low = pick(choices[:step], index, steps[:-1])
    high = pick(choices[step:], index, steps[:-1])
    return jnp.where((index & step) == 0, low, high)


def gather_blocks(block, axis, dim):
    count = lax.axis_size(axis)
    steps = bits_of(count)
    me = lax.axis_index(axis)
    pieces = {0: block}
    for step in reversed(steps):
        arrived = {key | step: swap(piece, axis, step) for key, piece in pieces.items()}
        pieces.update(arrived)
    listed = [pieces[key] for key in range(count)]
    ordered = [pick(listed, me ^ j, steps) for j in range(count)]
    return jnp.concatenate(ordered, axis=dim)


def reduce_blocks(partial_rows, axis, dim):
    count = lax.axis_size(axis)
    me = lax.axis_index(axis)
    width = partial_rows.shape[dim] // count
    held = [lax.slice_in_dim(partial_rows, j * width, (j + 1) * width, axis=dim) for j in range(count)]
    for step in bits_of(count):
        clear = (me & step) == 0
        kept = []
        for low, high in zip(held[0::2], held[1::2]):
            sent = jnp.where(clear, high, low).astype(BF16)
            kept.append((jnp.where(clear, low, high), swap(sent, axis, step)))
        held = [mine + theirs.astype(F32) for mine, theirs in kept]
    return held[0]


def norm_stats(tokens, gain, table):
    values = tokens.astype(F32)
    squares = jnp.sum(values * values, axis=1)[None, :]
    scores = lax.dot_general(
        (table * gain[:, None]), values, (((0,), (1,)), ((), ())), precision=HIGHEST
    )
    totals = butterfly_sum(jnp.concatenate([squares, scores], axis=0), "hid")
    return totals[0], totals[1:]


def finish_norm(tokens, squares, scores, gain, width):
    scale = lax.rsqrt(squares / width + EPSILON)
    normed = (tokens.astype(F32) * scale[:, None] * gain[None, :]).astype(BF16)
    return scale, normed, scores * scale[None, :]


def row_map(routes, rows):
    me = lax.axis_index("expert")
    tokens = routes.shape[1]
    hit = jnp.any(routes == me, axis=0)
    before = jnp.arange(tokens)[:, None] < jnp.arange(tokens)[None, :]
    rank = jnp.dot(hit.astype(BF16)[None, :], before.astype(BF16), preferred_element_type=F32)
    rank = rank.astype(jnp.int32)
    chosen = (jnp.arange(rows, dtype=jnp.int32)[:, None] == rank) & hit[None, :]
    return chosen


def pair_terms(routes, logits):
    experts = logits.shape[0]
    labels = jnp.arange(experts, dtype=jnp.int32)[:, None]
    first_hit = (routes[0:1] == labels).astype(F32)
    second_hit = (routes[1:2] == labels).astype(F32)
    first_logit = jnp.sum(logits * first_hit, axis=0)
    second_logit = jnp.sum(logits * second_hit, axis=0)
    first_prob = jax.nn.sigmoid(first_logit - second_logit)
    second_prob = jax.nn.sigmoid(second_logit - first_logit)
    return first_prob, second_prob, first_hit - second_hit


def per_row(chosen, per_token):
    return jnp.sum(jnp.where(chosen, per_token[None, :], 0.0), axis=1)


def select_rows(chosen, tokens):
    return jnp.dot(chosen.astype(BF16), tokens, preferred_element_type=F32).astype(BF16)


def send_home(chosen, rows):
    placed = lax.dot_general(
        chosen.astype(BF16), rows.astype(BF16), LEADING, preferred_element_type=F32
    )
    return reduce_blocks(placed, "expert", 0)


def per_device(
    saved_input,
    cotangent,
    next_input,
    routes_saved,
    routes_next,
    norm_gain,
    router,
    expert_gate,
    expert_up,
    expert_down,
):
    gain = norm_gain[0]
    table = router[0]
    gate_matrix = expert_gate[0, 0]
    up_matrix = expert_up[0, 0]
    down_matrix = expert_down[0, 0]
    width = gate_matrix.shape[0]
    count = saved_input.shape[1]
    rows = 3 * count * lax.axis_size("expert") // table.shape[1]
    me = lax.axis_index("expert")

    packed = jnp.concatenate([routes_saved[0].T, routes_next[0].T], axis=0)
    routes = gather_blocks(packed, "expert", 1)
    all_cot = gather_blocks(cotangent[0], "expert", 0)
    all_saved = gather_blocks(saved_input[0], "expert", 0)
    all_next = gather_blocks(next_input[0], "expert", 0)

    pair_saved, pair_next = routes[0:2], routes[2:4]
    chosen_saved = row_map(pair_saved, rows)
    chosen_next = row_map(pair_next, rows)

    cot_rows = gather_blocks(select_rows(chosen_saved, all_cot), "hid", 1)
    grad_hidden = lax.dot_general(cot_rows, down_matrix, CONTRACT, preferred_element_type=F32)

    squares, scores = norm_stats(all_saved, gain, table)
    scale_saved, normed, logits = finish_norm(all_saved, squares, scores, gain, width)
    first_saved, second_saved, diff_saved = pair_terms(pair_saved, logits)
    saved_rows = gather_blocks(select_rows(chosen_saved, normed), "hid", 1)

    squares, scores = norm_stats(all_next, gain, table)
    scale_next, normed, logits = finish_norm(all_next, squares, scores, gain, width)
    first_next, second_next, _ = pair_terms(pair_next, logits)
    next_rows = gather_blocks(select_rows(chosen_next, normed), "hid", 1)

    gate = jnp.dot(saved_rows, gate_matrix, preferred_element_type=F32)
    up = jnp.dot(saved_rows, up_matrix, preferred_element_type=F32)
    sig = jax.nn.sigmoid(gate)
    silu = gate * sig
    hidden = (silu * up).astype(BF16)
    dots = butterfly_sum(jnp.sum(grad_hidden * hidden.astype(F32), axis=1), "hid")
    grad_gate = (grad_hidden * up * (sig * (1.0 + gate * (1.0 - sig)))).astype(BF16)
    grad_up = (grad_hidden * silu).astype(BF16)
    back_part = lax.dot_general(
        grad_gate, gate_matrix, CONTRACT, preferred_element_type=F32
    ) + lax.dot_general(grad_up, up_matrix, CONTRACT, preferred_element_type=F32)
    back = reduce_blocks(back_part, "hid", 1)
    is_first = pair_saved[0] == me
    weight = per_row(chosen_saved, jnp.where(is_first, first_saved, second_saved))
    product = first_saved * second_saved
    slope = per_row(chosen_saved, jnp.where(is_first, product, -product)) * dots
    leaning = lax.dot_general(diff_saved * 1.0, table, (((0,), (1,)), ((), ())), precision=HIGHEST)
    spread = jnp.dot(chosen_saved.astype(F32), leaning, precision=HIGHEST)
    home = send_home(chosen_saved, weight[:, None] * back + slope[:, None] * spread)

    gate = jnp.dot(next_rows, gate_matrix, preferred_element_type=F32)
    up = jnp.dot(next_rows, up_matrix, preferred_element_type=F32)
    hidden = (gate * jax.nn.sigmoid(gate) * up).astype(BF16)
    out_part = jnp.dot(hidden, down_matrix, preferred_element_type=F32)
    out = reduce_blocks(out_part, "hid", 1)
    weight = per_row(chosen_next, jnp.where(pair_next[0] == me, first_next, second_next))
    branch = send_home(chosen_next, weight[:, None] * out)

    values_saved = saved_input[0].astype(F32)
    scaled_grad = home.astype(F32) * gain[None, :]
    inner = butterfly_sum(jnp.sum(scaled_grad * values_saved, axis=1), "hid")
    scale = lax.dynamic_slice(scale_saved, (me * count,), (count,))
    cube = scale * scale * scale
    grad_input = (
        cotangent[0].astype(F32)
        + scale[:, None] * scaled_grad
        - values_saved * cube[:, None] * (inner / width)[:, None]
    ).astype(BF16)
    forward_out = (next_input[0].astype(F32) + branch.astype(F32)).astype(BF16)

    first_section = lax.axis_index("section") == 0
    grad_there = one_way(grad_input, "section", 1, 0)
    out_there = one_way(forward_out, "section", 0, 1)
    leaving = jnp.where(first_section, grad_input, forward_out)
    arriving = jnp.where(first_section, grad_there, out_there)
    return (leaving[None], arriving[None])


def solution(mesh):
    placed = (
        P("section", "expert", "hid"),
        P("section", "expert", "hid"),
        P("section", "expert", "hid"),
        P("section", "expert", None),
        P("section", "expert", None),
        P("section", "hid"),
        P("section", "hid", None),
        P("section", "expert", None, "hid"),
        P("section", "expert", None, "hid"),
        P("section", "expert", "hid", None),
    )
    return jax.shard_map(
        per_device,
        mesh=mesh,
        in_specs=placed,
        out_specs=(P("section", "expert", "hid"), P("section", "expert", "hid")),
        check_vma=False,
    )
```
